32 devices in a mesh: layer: 4 (over y, core), feat: 8 (over z, x).
Axes of the slice: x: 2, y: 2, z: 4, core: 2. Of those that a mesh axis runs over, the one named last changes fastest.
Arguments:
- acts: bfloat16 [4, 384, 2048], P('layer', 'feat'), may hold values from -64 to 64
- errors: bfloat16 [4, 384, 2048], P('layer', 'feat'), may hold values from -2.390625 to 2.390625
- enc_weight: bfloat16 [4, 2048, 8192], P('layer', None, 'feat'), may hold values from -0.0625 to 0.0625
- dec_weight: bfloat16 [4, 8192, 2048], P('layer', 'feat'), may hold values from -0.125 to 0.125
- chosen: int32 [384, 32], replicated, may hold values from 0 to 8191, all different within a row
Outputs:
- dec_grad: bfloat16 [4, 8192, 2048], P('layer', 'feat')
- enc_grad: bfloat16 [4, 2048, 8192], P('layer', None, 'feat')
The draws below stay inside these ranges and needn't reach their ends.
Inputs may be any that keep to these rules, and one draw needn't show every extreme that they name: `chosen`: each row names 32 different features.
All inputs are finite; a program needn't handle non-finite values.
Results may differ from the reference program's by a relative error of at most 0.02.
Values may be sent and summed in bfloat16 or wider, within the bound.
No kernel may reach another device: no remote copies, remote signals or barrier semaphores. Data moves between devices by JAX's collectives and lax.ppermute only.
A program may use at most 64 MiB of HBM per device.

```python
import jax
import jax.numpy as jnp
from jax import lax

D = 2048
FEATURES = 8192
K = 32
LAYERS = 4
TOKENS = 384


def draw_acts(key, part):
    keys = jax.random.split(key, 2)
    position = jnp.arange(TOKENS, dtype=jnp.float32) / max(TOKENS - 1, 1)
    depth = jnp.exp(jnp.linspace(0.0, 0.7, LAYERS)).astype(jnp.float32)
    base = jnp.clip(jax.random.normal(keys[0], (LAYERS, TOKENS, D), jnp.float32), -4.0, 4.0)
    rough = jax.random.uniform(keys[1], (TOKENS,), jnp.float32, 0.7, 1.4)
    rising = 3.0 ** position
    scaled = base * (rising * rough)[None, :, None] * depth[:, None, None]
    return jnp.clip(scaled, -64.0, 64.0).astype(jnp.bfloat16)


def block_scale(own_key, extent, cuts, low, high):
    def one(dim, blocks):
        draws = jax.random.uniform(jax.random.fold_in(jax.random.fold_in(own_key, 6), dim), (blocks,), jnp.float32, low / len(cuts), high / len(cuts))
        return jnp.repeat(jnp.exp(draws), extent[dim] // blocks).reshape((-1,) + (1,) * (len(extent) - dim - 1))

    level = one(*cuts[0])
    for cut in cuts[1:]:
        level = level * one(*cut)
    return level


def different_ones(stream_key, rows, amount, top, lift):
    ranking = jax.random.permutation(jax.random.fold_in(stream_key, 1), amount)
    boost = ranking
    for power in range(3):
        boost = boost * boost // amount
    boost = boost * lift // amount
    lots = jax.random.randint(jax.random.fold_in(stream_key, 2), (rows, amount), 0, 4096) + boost
    fixed_rows = jax.random.permutation(jax.random.fold_in(stream_key, 3), rows)[jnp.arange(amount) % rows]
    lots = jnp.where(jnp.arange(rows)[:, None] == fixed_rows[None, :], 1 << 14, lots)
    merit = lots * amount + jnp.arange(amount)
    return lax.top_k(merit.astype(jnp.int32), top)[1].astype(jnp.int32)


def bell_draw(own_key, extent, scale, most, cuts=(), held_as=jnp.bfloat16):
    values = jax.random.normal(own_key, extent, jnp.float32) * scale
    if len(cuts) > 0:
        values = block_scale(own_key, extent, cuts, -0.22, 0.18) * values
    return jnp.clip(values, min=-most, max=most).astype(held_as)


def setup_inputs(seed: int = 0) -> dict:
    streams_of = jax.random.split(jax.random.key(seed), 6)
    acts = draw_acts(jax.random.fold_in(streams_of[5], 71), 0)
    errors = bell_draw(streams_of[1], (LAYERS, TOKENS, D), 0.3, 2.390625, ((0, 4), (1, 8)))
    enc_weight = bell_draw(streams_of[2], (LAYERS, D, FEATURES), (LAYERS * D) ** -0.5, 0.0625, ((0, 4), (2, 8)))
    dec_weight = bell_draw(streams_of[3], (LAYERS, FEATURES, D), D ** -0.5, 0.125, ((0, 4), (1, 8)))
    chosen = different_ones(streams_of[4], TOKENS, FEATURES, K, 32)
    return {"acts": acts, "errors": errors, "enc_weight": enc_weight, "dec_weight": dec_weight, "chosen": chosen}


def reference(acts, errors, enc_weight, dec_weight, chosen):

    def add_layer(total, pair):
        rows, weight = pair
        return (total + jnp.dot(rows, weight, preferred_element_type=jnp.float32), None)
    pre, _ = lax.scan(add_layer, jnp.zeros((TOKENS, FEATURES), jnp.float32), (acts, enc_weight))
    token_index = jnp.arange(TOKENS, dtype=jnp.int32)[:, None]
    mask = jnp.zeros((TOKENS, FEATURES), jnp.float32).at[token_index, chosen.astype(jnp.int32)].set(1.0)
    codes = (pre * mask).astype(jnp.bfloat16)
    mean_square = lax.optimization_barrier(jnp.mean(jnp.square(acts.astype(jnp.float32)), axis=(1, 2)))
    scale = 2.0 / (mean_square + 1e-06)
    delta = (errors.astype(jnp.float32) * scale[:, None, None]).astype(jnp.bfloat16)

    def layer_grads(total, pair):
        delta_rows, weight = pair
        grad = jnp.dot(codes.T, delta_rows, preferred_element_type=jnp.float32).astype(jnp.bfloat16)
        total = total + jnp.dot(delta_rows, weight.T, preferred_element_type=jnp.float32)
        return (total, grad)
    code_grad, dec_grad = lax.scan(layer_grads, jnp.zeros((TOKENS, FEATURES), jnp.float32), (delta, dec_weight))
    pre_grad = (code_grad * mask).astype(jnp.bfloat16)

    def encoder_grad(rows):
        return jnp.dot(rows.T, pre_grad, preferred_element_type=jnp.float32).astype(jnp.bfloat16)
    enc_grad = lax.map(encoder_grad, acts)
    return (dec_grad, enc_grad)
```

```python
import functools

import jax
import jax.numpy as jnp
from jax import lax
from jax.experimental import pallas as pl
from jax.experimental.pallas import tpu as pltpu
from jax.sharding import PartitionSpec as P

LANES = 128
SUB = 8
F32 = jnp.float32
BF16 = jnp.bfloat16


def scope(name):
    return jax.named_scope(name)


def index_kernel(starts, chosen, tgt, inv):
    tokens, width = inv.shape
    k = chosen.shape[1]
    per = LANES // k
    quarter = tokens // per
    first = starts[0]
    n_chunks = starts.shape[0] - 1
    rows = tokens // n_chunks
    for p in range(n_chunks):
        block = chosen[pl.ds(pl.multiple_of(starts[1 + p], SUB), rows), :] - first
        q, r0 = divmod(p * rows, quarter)
        tgt[r0 : r0 + rows, q * k : (q + 1) * k] = block
    column = lax.broadcasted_iota(jnp.int32, (SUB, width), 1)

    def body(m, _):
        ids = tgt[pl.ds(pl.multiple_of(m * SUB, SUB), SUB), :]
        for q in range(per):
            out = jnp.full((SUB, width), -1, jnp.int32)
            for j in range(k):
                lane = q * k + j
                out = jnp.where(ids[:, lane : lane + 1] == column, lane, out)
            inv[pl.ds(pl.multiple_of(q * quarter + m * SUB, SUB), SUB), :] = out
        return 0

    lax.fori_loop(0, quarter // SUB, body, 0)


def pick(dense, ids, out, block, k):
    tokens, width = dense.shape
    per = LANES // k
    quarter = tokens // per
    lane_group = lax.broadcasted_iota(jnp.int32, (SUB, LANES), 1) // k
    blocks = width // LANES
    for m in range(quarter // SUB):
        rows = slice(m * SUB, (m + 1) * SUB)
        want = ids[rows, :]
        low = jnp.bitwise_and(want, LANES - 1)
        key = (jnp.right_shift(want, 7) - block * blocks) * per + lane_group
        value = out[rows, :]
        for h in range(blocks):
            for q in range(per):
                t = q * quarter + m * SUB
                got = jnp.take_along_axis(
                    dense[t : t + SUB, h * LANES : (h + 1) * LANES], low, axis=1
                )
                value = jnp.where(key == h * per + q, got, value)
        out[rows, :] = value


def expand(vals, inv, tokens, k):
    per = LANES // k
    quarter = tokens // per
    width = inv.shape[1]
    rows_out = []
    for t in range(0, tokens, SUB):
        m = t % quarter
        source = vals[m : m + SUB, :]
        parts = []
        for h in range(width // LANES):
            at = inv[t : t + SUB, h * LANES : (h + 1) * LANES]
            got = jnp.take_along_axis(source, jnp.bitwise_and(at, LANES - 1), axis=1)
            parts.append(jnp.where(at >= 0, got, 0.0))
        rows_out.append(jnp.concatenate(parts, axis=1))
    return jnp.concatenate(rows_out, axis=0)


def pre_kernel(n_chunks, k, *refs):
    chunks = refs[:n_chunks]
    weight, tgt, vals, scale, turned, all_rows, dense, acc = refs[n_chunks:]
    step = pl.program_id(0)
    rows = chunks[0].shape[1]

    @pl.when(step == 0)
    def _():
        acc[...] = jnp.zeros_like(acc)
        for p in range(n_chunks):
            all_rows[p * rows : (p + 1) * rows, :] = chunks[p][0]

    dense[...] = jnp.dot(all_rows[...], weight[0], preferred_element_type=F32)
    pick(dense, tgt, acc, step, k)

    @pl.when(step == pl.num_programs(0) - 1)
    def _():
        vals[...] = acc[...].astype(BF16)
        values = all_rows[...].astype(F32)
        total = jnp.sum(values * values)
        mean = total / (all_rows.shape[0] * all_rows.shape[1])
        scale[...] = jnp.full(scale.shape, 2.0 / (mean + 1e-6), F32)
        turned[...] = all_rows[...].T


def code_grad_kernel(n_chunks, k, *refs):
    chunks = refs[:n_chunks]
    weight, tgt, scale, vals, all_rows, dense, acc = refs[n_chunks:]
    step = pl.program_id(0)
    rows = chunks[0].shape[1]

    @pl.when(step == 0)
    def _():
        acc[...] = jnp.zeros_like(acc)
        for p in range(n_chunks):
            all_rows[p * rows : (p + 1) * rows, :] = chunks[p][0]

    dense[...] = lax.dot_general(
        all_rows[...], weight[0], (((1,), (1,)), ((), ())), preferred_element_type=F32
    )
    pick(dense, tgt, acc, step, k)

    @pl.when(step == pl.num_programs(0) - 1)
    def _():
        vals[...] = (acc[...] * scale[0:1, 0:1]).astype(BF16)


def total_of(parts):
    total = parts[0][...].astype(F32)
    for part in parts[1:]:
        total = total + part[...].astype(F32)
    return total


def dec_grad_kernel(n_chunks, n_parts, k, *refs):
    chunks = refs[:n_chunks]
    parts = refs[n_chunks : n_chunks + n_parts]
    inv, scale, out, all_rows, vals = refs[n_chunks + n_parts :]
    rows = chunks[0].shape[1]

    @pl.when(pl.program_id(0) == 0)
    def _():
        vals[...] = total_of(parts)
        for p in range(n_chunks):
            all_rows[p * rows : (p + 1) * rows, :] = chunks[p][0]

    codes = expand(vals, inv, inv.shape[0], k)
    turned = codes.T.astype(BF16)
    grad = jnp.dot(turned, all_rows[...], preferred_element_type=F32)
    out[0] = (grad * scale[0:1, 0:1]).astype(BF16)


def enc_grad_kernel(n_parts, k, *refs):
    parts = refs[:n_parts]
    turned, inv, out, vals = refs[n_parts:]

    @pl.when(pl.program_id(0) == 0)
    def _():
        vals[...] = total_of(parts)

    pre_grad = expand(vals, inv, inv.shape[0], k).astype(BF16)
    out[0] = jnp.dot(turned[...], pre_grad, preferred_element_type=F32).astype(BF16)


def whole(shape):
    return pl.BlockSpec(shape, lambda i: (0,) * len(shape))


def call(kernel, grid, in_specs, out_specs, out_shape, scratch, flops, nbytes, name):
    return pl.pallas_call(
        kernel,
        grid=(grid,),
        in_specs=in_specs,
        out_specs=out_specs,
        out_shape=out_shape,
        scratch_shapes=scratch,
        compiler_params=pltpu.CompilerParams(dimension_semantics=("arbitrary",)),
        cost_estimate=pl.CostEstimate(
            flops=flops, bytes_accessed=nbytes, transcendentals=0
        ),
        name=name,
    )


def on_device(outer, inner, n_layer, acts, errors, enc_weight, dec_weight, chosen):
    feat = outer * inner
    rows, width = acts.shape[1], acts.shape[2]
    feat_dev = enc_weight.shape[2]
    tokens, k = chosen.shape
    quarter = tokens // (LANES // k)
    me = lax.axis_index("feat")
    my_outer, my_inner = me // inner, me % inner
    ring = [
        (o * inner + i, ((o + 1) % outer) * inner + i)
        for o in range(outer)
        for i in range(inner)
    ]
    turns = [
        [(o * inner + i, o * inner + (i + c) % inner) for o in range(outer) for i in range(inner)]
        for c in range(inner)
    ]

    def gather(x, tag):
        held, chunks = x, []
        for step in range(outer):
            if step:
                with scope(f"ring_{tag}{step}"):
                    held = lax.ppermute(held, "feat", ring)
            chunks.append(held)
            for c in range(1, inner):
                with scope(f"side_{tag}{step}"):
                    chunks.append(lax.ppermute(held, "feat", turns[c]))
        return chunks

    starts = [me * feat_dev]
    for step in range(outer):
        for c in range(inner):
            o = (my_outer - step + outer) % outer
            i = (my_inner - c + inner) % inner
            starts.append((o * inner + i) * rows)
    starts = jnp.stack(starts).astype(jnp.int32)

    a = gather(acts, "a")
    e = gather(errors, "e")

    tgt, inv = pl.pallas_call(
        index_kernel,
        in_specs=[pl.BlockSpec(memory_space=pltpu.SMEM), pl.BlockSpec(memory_space=pltpu.VMEM)],
        out_specs=[pl.BlockSpec(memory_space=pltpu.VMEM)] * 2,
        out_shape=[
            jax.ShapeDtypeStruct((quarter, LANES), jnp.int32),
            jax.ShapeDtypeStruct((tokens, feat_dev), jnp.int32),
        ],
        cost_estimate=pl.CostEstimate(
            flops=tokens * k * feat_dev, bytes_accessed=4 * tokens * feat_dev, transcendentals=0
        ),
        name="index",
    )(starts, chosen)

    block = min(256, feat_dev)
    steps = feat_dev // block
    flops = 2 * tokens * width * feat_dev
    nbytes = 2 * width * feat_dev
    chunk_spec = whole((1, rows, width))
    packed_bf = jax.ShapeDtypeStruct((quarter, LANES), BF16)
    row_scratch = pltpu.VMEM((tokens, width), BF16)

    def exchange(value, tag):
        parts = [value]
        for s in range(1, n_layer):
            pairs = [(d, (d + s) % n_layer) for d in range(n_layer)]
            with scope(f"swap_{tag}{s}"):
                parts.append(lax.ppermute(value, "layer", pairs))
        return parts

    vals, scale, turned = call(
        functools.partial(pre_kernel, feat, k),
        steps,
        [chunk_spec] * feat
        + [pl.BlockSpec((1, width, block), lambda i: (0, 0, i)), whole((quarter, LANES))],
        [whole((quarter, LANES)), whole((SUB, LANES)), whole((width, tokens))],
        [packed_bf, jax.ShapeDtypeStruct((SUB, LANES), F32), jax.ShapeDtypeStruct((width, tokens), BF16)],
        [row_scratch, pltpu.VMEM((tokens, block), F32), pltpu.VMEM((quarter, LANES), F32)],
        flops, nbytes, "pre",
    )(*a, enc_weight, tgt)
    pre_parts = exchange(vals, "p")

    vals = call(
        functools.partial(code_grad_kernel, feat, k),
        steps,
        [chunk_spec] * feat
        + [pl.BlockSpec((1, block, width), lambda i: (0, i, 0)), whole((quarter, LANES)), whole((SUB, LANES))],
        whole((quarter, LANES)),
        packed_bf,
        [row_scratch, pltpu.VMEM((tokens, block), F32), pltpu.VMEM((quarter, LANES), F32)],
        flops, nbytes, "code_grad",
    )(*e, dec_weight, tgt, scale)
    grad_parts = exchange(vals, "g")

    inv_spec = pl.BlockSpec((tokens, block), lambda i: (0, i))
    dec_grad = call(
        functools.partial(dec_grad_kernel, feat, n_layer, k),
        steps,
        [chunk_spec] * feat + [whole((quarter, LANES))] * n_layer + [inv_spec, whole((SUB, LANES))],
        pl.BlockSpec((1, block, width), lambda i: (0, i, 0)),
        jax.ShapeDtypeStruct((1, feat_dev, width), BF16),
        [row_scratch, pltpu.VMEM((quarter, LANES), F32)],
        flops, nbytes, "dec_grad",
    )(*e, *pre_parts, inv, scale)
    enc_grad = call(
        functools.partial(enc_grad_kernel, n_layer, k),
        steps,
        [whole((quarter, LANES))] * n_layer + [whole((width, tokens)), inv_spec],
        pl.BlockSpec((1, width, block), lambda i: (0, 0, i)),
        jax.ShapeDtypeStruct((1, width, feat_dev), BF16),
        [pltpu.VMEM((quarter, LANES), F32)],
        flops, nbytes, "enc_grad",
    )(*grad_parts, turned, inv)
    return (dec_grad, enc_grad)


def solution(mesh):
    feat, n_layer = mesh.shape["feat"], mesh.shape["layer"]
    inner = 2 if feat % 2 == 0 else 1
    return jax.shard_map(
        functools.partial(on_device, feat // inner, inner, n_layer),
        mesh=mesh,
        in_specs=(
            P("layer", "feat", None),
            P("layer", "feat", None),
            P("layer", None, "feat"),
            P("layer", "feat", None),
            P(),
        ),
        out_specs=(P("layer", "feat", None), P("layer", None, "feat")),
        check_vma=False,
    )
```

```python
import functools

import jax
import jax.numpy as jnp
from jax import lax
from jax.experimental import pallas as pl
from jax.experimental.pallas import tpu as pltpu
from jax.sharding import PartitionSpec as P


LANES = 128
VECTOR_FLOPS = 1024
SUB = 8
F32 = jnp.float32
BF16 = jnp.bfloat16


def pack_kernel(starts, chosen, tgt, held):
    k, tokens = chosen.shape
    quarter = tgt.shape[0]
    n_chunks = starts.shape[0] - 1
    rows = tokens // n_chunks
    held[:, :k] = chosen[...].T - starts[0]
    for p in range(n_chunks):
        q, r0 = divmod(p * rows, quarter)
        tgt[r0 : r0 + rows, q * k : (q + 1) * k] = held[pl.ds(pl.multiple_of(starts[1 + p], SUB), rows), :k]


def index_kernel(k, groups, tgt, inv):
    width = inv.shape[1]
    quarter = tgt.shape[0]
    column = lax.broadcasted_iota(jnp.int32, (SUB, width), 1)

    def body(m, _):
        ids = tgt[pl.ds(pl.multiple_of(m * SUB, SUB), SUB), :]
        for n, q in enumerate(groups):
            out = jnp.full((SUB, width), -1, jnp.int32)
            for j in range(k):
                lane = q * k + j
                out = jnp.where(ids[:, lane : lane + 1] == column, lane, out)
            inv[pl.ds(pl.multiple_of(n * quarter + m * SUB, SUB), SUB), :] = out
        return 0

    lax.fori_loop(0, quarter // SUB, body, 0)


def pick(dense, ids, out, groups, first_block, k):
    width = dense.shape[1]
    per = LANES // k
    quarter = ids.shape[0]
    lane_group = lax.broadcasted_iota(jnp.int32, (SUB, LANES), 1) // k
    blocks = width // LANES
    picked = []
    for m in range(quarter // SUB):
        want = ids[m * SUB : (m + 1) * SUB, :]
        low = jnp.bitwise_and(want, LANES - 1)
        key = jnp.right_shift(want, 7) * per + lane_group
        value = out[m]
        for h in range(blocks):
            for q in groups:
                t = (q - groups[0]) * quarter + m * SUB
                got = jnp.take_along_axis(
                    dense[t : t + SUB, h * LANES : (h + 1) * LANES], low, axis=1
                )
                value = jnp.where(key == (first_block + h) * per + q, got, value)
        picked.append(value)
    return picked


def expand(vals, inv, first, size):
    tokens = inv.shape[0]
    quarter = vals[0].shape[0] * len(vals)
    rows_out = []
    for t in range(0, tokens, SUB):
        source = vals[t % quarter // SUB]
        parts = []
        for h in range(size // LANES):
            at = inv[t : t + SUB, first + h * LANES : first + (h + 1) * LANES]
            got = jnp.take_along_axis(source, jnp.bitwise_and(at, LANES - 1), axis=1)
            parts.append(jnp.where(at >= 0, got, 0.0))
        rows_out.append(jnp.concatenate(parts, axis=1))
    return jnp.concatenate(rows_out, axis=0)


def row_blocks(ref):
    return [ref[m : m + SUB, :] for m in range(0, ref.shape[0], SUB)]


def stacked(chunks):
    return jnp.concatenate([chunk[0] for chunk in chunks], axis=0)


def pre_kernel(n_chunks, groups, k, block, *refs):
    chunks = refs[:n_chunks]
    weight, ids, vals = refs[n_chunks:]
    rows = stacked(chunks)
    acc = [jnp.zeros((SUB, LANES), F32)] * (ids.shape[0] // SUB)
    for j in range(0, weight.shape[2], block):
        dense = jnp.dot(rows, weight[0, :, j : j + block], preferred_element_type=F32)
        acc = pick(dense, ids, acc, groups, j // LANES, k)
    vals[...] = jnp.concatenate(acc, axis=0).astype(vals.dtype)


def turn_kernel(n_chunks, *refs):
    chunks = refs[:n_chunks]
    squares, turned = refs[n_chunks:]
    rows = stacked(chunks)
    turned[...] = rows.T
    tokens, width = rows.shape
    values = rows.astype(F32)
    total = jnp.sum((values * values).reshape(tokens // SUB, SUB, width), axis=0)
    part = total[:, :LANES]
    for j in range(LANES, width, LANES):
        part = part + total[:, j : j + LANES]
    squares[...] = part


def scale_of(squares, count):
    return 2.0 / (jnp.sum(squares[...]) / count + 1e-6)


def code_grad_kernel(n_chunks, groups, k, block, first, last, count, *refs):
    refs = list(refs)
    chunks = [refs.pop(0) for _ in range(n_chunks)]
    weight, ids = refs.pop(0), refs.pop(0)
    before = None if first else refs.pop(0)
    squares = refs.pop(0) if last else None
    (vals,) = refs
    rows = stacked(chunks)
    quarter = ids.shape[0]
    acc = [jnp.zeros((SUB, LANES), F32)] * (quarter // SUB) if first else row_blocks(before)
    for j in range(0, weight.shape[1], block):
        dense = lax.dot_general(
            rows, weight[0, j : j + block, :], (((1,), (1,)), ((), ())), preferred_element_type=F32
        )
        acc = pick(dense, ids, acc, groups, j // LANES, k)
    out = jnp.concatenate(acc, axis=0)
    if last:
        out = out * scale_of(squares, count)
    vals[...] = out.astype(vals.dtype)


def total_of(parts):
    total = parts[0][...].astype(F32)
    for part in parts[1:]:
        total = total + part[...].astype(F32)
    return total


def split_rows(value):
    return [value[m : m + SUB] for m in range(0, value.shape[0], SUB)]


def dec_grad_kernel(n_chunks, n_parts, block, count, *refs):
    chunks = refs[:n_chunks]
    parts = refs[n_chunks : n_chunks + n_parts]
    *inv, squares, out, held, sems = refs[n_chunks + n_parts :]
    vals = split_rows(total_of(parts) * scale_of(squares, count))
    rows = stacked(chunks)
    copies = []
    for n, j in enumerate(range(0, inv[0].shape[1], block)):
        codes = jnp.concatenate([expand(vals, half, j, block) for half in inv], axis=0).T.astype(BF16)
        held[j : j + block, :] = jnp.dot(codes, rows, preferred_element_type=F32).astype(BF16)
        copies.append(
            pltpu.make_async_copy(held.at[pl.ds(j, block), :], out.at[0, pl.ds(j, block), :], sems.at[n])
        )
        copies[-1].start()
    for copy in copies:
        copy.wait()


def enc_grad_kernel(n_parts, block, tall, *refs):
    parts = refs[:n_parts]
    turned, *inv, out, held, sems = refs[n_parts:]
    vals = split_rows(total_of(parts))
    copies = []
    for n, j in enumerate(range(0, inv[0].shape[1], block)):
        pre_grad = jnp.concatenate([expand(vals, half, j, block) for half in inv], axis=0).astype(BF16)
        for m in range(0, turned.shape[0], tall):
            held[m : m + tall, j : j + block] = jnp.dot(
                turned[m : m + tall, :], pre_grad, preferred_element_type=F32
            ).astype(BF16)
        copies.append(
            pltpu.make_async_copy(held.at[:, pl.ds(j, block)], out.at[0, :, pl.ds(j, block)], sems.at[n])
        )
        copies[-1].start()
    for copy in copies:
        copy.wait()


VMEM = pl.BlockSpec(memory_space=pltpu.VMEM)
SMEM = pl.BlockSpec(memory_space=pltpu.SMEM)
ANY = pl.BlockSpec(memory_space=pl.ANY)


def call(kernel, args, in_specs, out_specs, out_shape, scratch, flops, nbytes):
    return pl.pallas_call(
        kernel,
        in_specs=in_specs,
        out_specs=out_specs,
        out_shape=out_shape,
        scratch_shapes=scratch,
        compiler_params=pltpu.CompilerParams(vmem_limit_bytes=24 << 20),
        cost_estimate=pl.CostEstimate(
            flops=flops, bytes_accessed=nbytes, transcendentals=0
        ),
    )(*args)


def on_device_ops(outer, inner, n_layer, acts, errors, enc_weight, dec_weight, chosen):
    feat = outer * inner
    rows, width = acts.shape[1], acts.shape[2]
    feat_dev = enc_weight.shape[2]
    tokens, k = chosen.shape
    quarter = tokens // (LANES // k)
    me = lax.axis_index("feat")
    my_outer, my_inner = me // inner, me % inner
    places = [(o, i) for o in range(outer) for i in range(inner)]

    def ring(by):
        return [(o * inner + i, (o + by) % outer * inner + i) for o, i in places]

    def turn(by):
        return [(o * inner + i, o * inner + (i + by) % inner) for o, i in places]

    def send(x, pairs):
        return lax.ppermute(x, "feat", pairs)

    right, left = steps_of(outer)

    def gather(x, last_by_ring):
        fronts, sides = [x], [[send(x, turn(c)) for c in range(1, inner)]]
        for n in range(1, right + 1):
            fronts.append(send(fronts[-1], ring(1)))
            if n == right and last_by_ring:
                sides.append([send(y, ring(1)) for y in sides[-1]])
            else:
                sides.append([send(fronts[-1], turn(c)) for c in range(1, inner)])
        held = x
        for _ in range(1, left + 1):
            held = send(held, ring(-1))
            fronts.append(held)
            sides.append([send(held, turn(c)) for c in range(1, inner)])
        return [y for front, side in zip(fronts, sides) for y in (front, *side)]

    starts = [me * feat_dev]
    for by in [*range(right + 1), *(-n for n in range(1, left + 1))]:
        for c in range(inner):
            o = (my_outer - by + outer) % outer
            i = (my_inner - c + inner) % inner
            starts.append((o * inner + i) * rows)
    starts = jnp.stack(starts).astype(jnp.int32)

    a = gather(acts, False)
    e = gather(errors, True)

    shape = jax.ShapeDtypeStruct
    per = LANES // k
    block = min(256, feat_dev)
    tgt = call(
        pack_kernel, (starts, chosen.T), [SMEM, VMEM], VMEM,
        shape((quarter, LANES), jnp.int32), [pltpu.VMEM((tokens, LANES), jnp.int32)],
        tokens * k, 4 * tokens * LANES,
    )
    halves = [tuple(range(per // 2)), tuple(range(per // 2, per))]
    per_half = feat // 2
    half_tokens = tokens // 2
    half_flops = 2 * half_tokens * width * feat_dev
    half_bytes = 2 * width * half_tokens
    inv = []
    for groups in halves:
        inv.append(
            call(
                functools.partial(index_kernel, k, groups), (tgt,), [VMEM], VMEM,
                shape((half_tokens, feat_dev), jnp.int32), [],
                VECTOR_FLOPS * half_tokens * k * feat_dev, 4 * half_tokens * feat_dev,
            )
        )

    def exchange(value):
        parts = [value]
        for s in range(1, n_layer):
            pairs = [(d, (d + s) % n_layer) for d in range(n_layer)]
            parts.append(lax.ppermute(value, "layer", pairs))
        return parts

    args = (*a, enc_weight, tgt)
    vals = call(
        functools.partial(pre_kernel, feat, tuple(range(per)), k, block),
        args, [VMEM] * len(args), VMEM, shape((quarter, LANES), BF16),
        [], 2 * half_flops, 2 * half_bytes,
    )
    squares, turned = call(
        functools.partial(turn_kernel, feat), a, [VMEM] * feat, [VMEM, VMEM],
        [shape((SUB, LANES), F32), shape((width, tokens), BF16)],
        [], 2 * tokens * width, 4 * half_bytes,
    )
    pre_parts = exchange(vals)

    vals = []
    for n, groups in enumerate(halves):
        first, last = n == 0, n == len(halves) - 1
        args = (*e[n * per_half : (n + 1) * per_half], dec_weight, tgt, *vals, *([squares] if last else []))
        vals = [
            call(
                functools.partial(
                    code_grad_kernel, per_half, groups, k, block, first, last, tokens * width
                ),
                args, [VMEM] * len(args), VMEM, shape((quarter, LANES), BF16 if last else F32),
                [], half_flops, half_bytes,
            )
        ]
    grad_parts = exchange(vals[0])

    def out_scratch(rows, columns):
        return [pltpu.VMEM((rows, columns), BF16), pltpu.SemaphoreType.DMA((feat_dev // block,))]

    args = (*e, *pre_parts, *inv, squares)
    dec_grad = call(
        functools.partial(dec_grad_kernel, feat, n_layer, block, tokens * width),
        args, [VMEM] * len(args), ANY, shape((1, feat_dev, width), BF16),
        out_scratch(feat_dev, width), 2 * half_flops, 2 * feat_dev * width,
    )
    args = (*grad_parts, turned, *inv)
    enc_grad = call(
        functools.partial(enc_grad_kernel, n_layer, block, min(512, width)),
        args, [VMEM] * len(args), ANY, shape((1, width, feat_dev), BF16),
        out_scratch(width, feat_dev), 2 * half_flops, 2 * feat_dev * width,
    )
    return (dec_grad, enc_grad)


def steps_of(outer):
    return outer // 2, outer - 1 - outer // 2


def solution(mesh):
    feat, n_layer = mesh.shape["feat"], mesh.shape["layer"]
    inner = 2 if feat % 2 == 0 else 1

    return jax.shard_map(
        functools.partial(on_device_ops, feat // inner, inner, n_layer),
        mesh=mesh,
        in_specs=(
            P("layer", "feat", None),
            P("layer", "feat", None),
            P("layer", None, "feat"),
            P("layer", "feat", None),
            P(),
        ),
        out_specs=(P("layer", "feat", None), P("layer", None, "feat")),
        check_vma=False,
    )
```

```python
import functools

import jax
import jax.numpy as jnp
from jax import lax
from jax.experimental import pallas as pl
from jax.experimental.pallas import tpu as pltpu
from jax.sharding import PartitionSpec as P


LANES = 128
VECTOR_FLOPS = 1024
SUB = 8
F32 = jnp.float32
BF16 = jnp.bfloat16


def lanes_of(x, index):
    numbers = lax.GatherDimensionNumbers(
        offset_dims=(),
        collapsed_slice_dims=(1,),
        start_index_map=(1,),
        operand_batching_dims=(0,),
        start_indices_batching_dims=(0,),
    )
    return lax.gather(
        x, index[..., None], numbers, slice_sizes=(1, 1), mode=lax.GatherScatterMode.PROMISE_IN_BOUNDS
    )


def pack_kernel(starts, chosen, tgt, held):
    k, tokens = chosen.shape
    quarter = tgt.shape[0]
    n_chunks = starts.shape[0] - 1
    rows = tokens // n_chunks
    held[:, :k] = chosen[...].T - starts[0]
    for p in range(n_chunks):
        q, r0 = divmod(p * rows, quarter)
        tgt[r0 : r0 + rows, q * k : (q + 1) * k] = held[pl.ds(pl.multiple_of(starts[1 + p], SUB), rows), :k]


def index_kernel(k, groups, tgt, inv):
    width = inv.shape[1]
    quarter = tgt.shape[0]
    column = lax.broadcasted_iota(jnp.int32, (SUB, width), 1)

    def body(m, _):
        ids = tgt[pl.ds(pl.multiple_of(m * SUB, SUB), SUB), :]
        for n, q in enumerate(groups):
            out = jnp.full((SUB, width), -1, jnp.int32)
            for j in range(k):
                lane = q * k + j
                out = jnp.where(ids[:, lane : lane + 1] == column, lane, out)
            inv[pl.ds(pl.multiple_of(n * quarter + m * SUB, SUB), SUB), :] = out
        return 0

    lax.fori_loop(0, quarter // SUB, body, 0)


def pick(dense, ids, out, groups, first_block, k):
    width = dense.shape[1]
    per = LANES // k
    quarter = ids.shape[0]
    lane_group = lax.broadcasted_iota(jnp.int32, (SUB, LANES), 1) // k
    blocks = width // LANES
    picked = []
    for m in range(quarter // SUB):
        want = ids[m * SUB : (m + 1) * SUB, :]
        low = jnp.bitwise_and(want, LANES - 1)
        key = jnp.right_shift(want, 7) * per + lane_group
        value = out[m]
        for h in range(blocks):
            for q in groups:
                t = (q - groups[0]) * quarter + m * SUB
                got = lanes_of(dense[t : t + SUB, h * LANES : (h + 1) * LANES], low)
                value = jnp.where(key == (first_block + h) * per + q, got, value)
        picked.append(value)
    return picked


def expand(vals, inv, first, size):
    tokens = inv.shape[0]
    quarter = vals[0].shape[0] * len(vals)
    rows_out = []
    for t in range(0, tokens, SUB):
        source = vals[t % quarter // SUB]
        parts = []
        for h in range(size // LANES):
            at = inv[t : t + SUB, first + h * LANES : first + (h + 1) * LANES]
            got = lanes_of(source, jnp.bitwise_and(at, LANES - 1))
            parts.append(jnp.where(at >= 0, got, 0.0))
        rows_out.append(jnp.concatenate(parts, axis=1))
    return jnp.concatenate(rows_out, axis=0)


def row_blocks(ref):
    return [ref[m : m + SUB, :] for m in range(0, ref.shape[0], SUB)]


def stacked(chunks):
    return jnp.concatenate([chunk[0] for chunk in chunks], axis=0)


def pre_kernel(n_chunks, groups, k, block, *refs):
    chunks = refs[:n_chunks]
    weight, ids, vals = refs[n_chunks:]
    rows = stacked(chunks)
    acc = [jnp.zeros((SUB, LANES), F32)] * (ids.shape[0] // SUB)
    for j in range(0, weight.shape[2], block):
        dense = jnp.dot(rows, weight[0, :, j : j + block], preferred_element_type=F32)
        acc = pick(dense, ids, acc, groups, j // LANES, k)
    vals[...] = jnp.concatenate(acc, axis=0).astype(vals.dtype)


def turn_kernel(n_chunks, *refs):
    chunks = refs[:n_chunks]
    squares, turned = refs[n_chunks:]
    rows = stacked(chunks)
    turned[...] = rows.T
    tokens, width = rows.shape
    values = rows.astype(F32)
    total = jnp.sum((values * values).reshape(tokens // SUB, SUB, width), axis=0)
    part = total[:, :LANES]
    for j in range(LANES, width, LANES):
        part = part + total[:, j : j + LANES]
    squares[...] = part


def scale_of(squares, count):
    return 2.0 / (jnp.sum(squares[...]) / count + 1e-6)


def code_grad_kernel(n_chunks, groups, k, block, first, last, count, *refs):
    refs = list(refs)
    chunks = [refs.pop(0) for _ in range(n_chunks)]
    weight, ids = refs.pop(0), refs.pop(0)
    before = None if first else refs.pop(0)
    squares = refs.pop(0) if last else None
    (vals,) = refs
    rows = stacked(chunks)
    quarter = ids.shape[0]
    acc = [jnp.zeros((SUB, LANES), F32)] * (quarter // SUB) if first else row_blocks(before)
    for j in range(0, weight.shape[1], block):
        dense = lax.dot_general(
            rows, weight[0, j : j + block, :], (((1,), (1,)), ((), ())), preferred_element_type=F32
        )
        acc = pick(dense, ids, acc, groups, j // LANES, k)
    out = jnp.concatenate(acc, axis=0)
    if last:
        out = out * scale_of(squares, count)
    vals[...] = out.astype(vals.dtype)


def total_of(parts):
    total = parts[0][...].astype(F32)
    for part in parts[1:]:
        total = total + part[...].astype(F32)
    return total


def split_rows(value):
    return [value[m : m + SUB] for m in range(0, value.shape[0], SUB)]


def dec_grad_kernel(n_chunks, n_parts, block, count, *refs):
    chunks = refs[:n_chunks]
    parts = refs[n_chunks : n_chunks + n_parts]
    *inv, squares, out, held, sems = refs[n_chunks + n_parts :]
    vals = split_rows(total_of(parts) * scale_of(squares, count))
    rows = stacked(chunks)
    copies = []
    for n, j in enumerate(range(0, inv[0].shape[1], block)):
        codes = jnp.concatenate([expand(vals, half, j, block) for half in inv], axis=0).T.astype(BF16)
        held[j : j + block, :] = jnp.dot(codes, rows, preferred_element_type=F32).astype(BF16)
        copies.append(
            pltpu.make_async_copy(held.at[pl.ds(j, block), :], out.at[0, pl.ds(j, block), :], sems.at[n])
        )
        copies[-1].start()
    for copy in copies:
        copy.wait()


def enc_grad_kernel(n_parts, block, tall, *refs):
    parts = refs[:n_parts]
    turned, *inv, out, held, sems = refs[n_parts:]
    vals = split_rows(total_of(parts))
    copies = []
    for n, j in enumerate(range(0, inv[0].shape[1], block)):
        pre_grad = jnp.concatenate([expand(vals, half, j, block) for half in inv], axis=0).astype(BF16)
        for m in range(0, turned.shape[0], tall):
            held[m : m + tall, j : j + block] = jnp.dot(
                turned[m : m + tall, :], pre_grad, preferred_element_type=F32
            ).astype(BF16)
        copies.append(
            pltpu.make_async_copy(held.at[:, pl.ds(j, block)], out.at[0, :, pl.ds(j, block)], sems.at[n])
        )
        copies[-1].start()
    for copy in copies:
        copy.wait()


VMEM = pl.BlockSpec(memory_space=pltpu.VMEM)
SMEM = pl.BlockSpec(memory_space=pltpu.SMEM)
ANY = pl.BlockSpec(memory_space=pl.ANY)


def call(kernel, args, in_specs, out_specs, out_shape, scratch, flops, nbytes):
    return pl.pallas_call(
        kernel,
        in_specs=in_specs,
        out_specs=out_specs,
        out_shape=out_shape,
        scratch_shapes=scratch,
        compiler_params=pltpu.CompilerParams(vmem_limit_bytes=24 << 20),
        cost_estimate=pl.CostEstimate(
            flops=flops, bytes_accessed=nbytes, transcendentals=0
        ),
    )(*args)


def on_device_ops(outer, inner, n_layer, acts, errors, enc_weight, dec_weight, chosen):
    feat = outer * inner
    rows, width = acts.shape[1], acts.shape[2]
    feat_dev = enc_weight.shape[2]
    tokens, k = chosen.shape
    quarter = tokens // (LANES // k)
    me = lax.axis_index("feat")
    my_outer, my_inner = me // inner, me % inner
    places = [(o, i) for o in range(outer) for i in range(inner)]

    def ring(by):
        return [(o * inner + i, (o + by) % outer * inner + i) for o, i in places]

    def turn(by):
        return [(o * inner + i, o * inner + (i + by) % inner) for o, i in places]

    def send(x, pairs):
        return lax.ppermute(x, "feat", pairs)

    right, left = steps_of(outer)

    def gather(x, last_by_ring):
        fronts, sides = [x], [[send(x, turn(c)) for c in range(1, inner)]]
        for n in range(1, right + 1):
            fronts.append(send(fronts[-1], ring(1)))
            if n == right and last_by_ring:
                sides.append([send(y, ring(1)) for y in sides[-1]])
            else:
                sides.append([send(fronts[-1], turn(c)) for c in range(1, inner)])
        held = x
        for _ in range(1, left + 1):
            held = send(held, ring(-1))
            fronts.append(held)
            sides.append([send(held, turn(c)) for c in range(1, inner)])
        return [y for front, side in zip(fronts, sides) for y in (front, *side)]

    starts = [me * feat_dev]
    for by in [*range(right + 1), *(-n for n in range(1, left + 1))]:
        for c in range(inner):
            o = (my_outer - by + outer) % outer
            i = (my_inner - c + inner) % inner
            starts.append((o * inner + i) * rows)
    starts = jnp.stack(starts).astype(jnp.int32)

    a = gather(acts, False)
    e = gather(errors, True)

    shape = jax.ShapeDtypeStruct
    per = LANES // k
    block = min(256, feat_dev)
    tgt = call(
        pack_kernel, (starts, chosen.T), [SMEM, VMEM], VMEM,
        shape((quarter, LANES), jnp.int32), [pltpu.VMEM((tokens, LANES), jnp.int32)],
        tokens * k, 4 * tokens * LANES,
    )
    halves = [tuple(range(per // 2)), tuple(range(per // 2, per))]
    per_half = feat // 2
    half_tokens = tokens // 2
    half_flops = 2 * half_tokens * width * feat_dev
    half_bytes = 2 * width * half_tokens
    inv = []
    for groups in halves:
        inv.append(
            call(
                functools.partial(index_kernel, k, groups), (tgt,), [VMEM], VMEM,
                shape((half_tokens, feat_dev), jnp.int32), [],
                VECTOR_FLOPS * half_tokens * k * feat_dev, 4 * half_tokens * feat_dev,
            )
        )

    def exchange(value):
        parts = [value]
        for s in range(1, n_layer):
            pairs = [(d, partner(d, s, n_layer)) for d in range(n_layer)]
            parts.append(lax.ppermute(value, "layer", pairs))
        return parts

    args = (*a, enc_weight, tgt)
    vals = call(
        functools.partial(pre_kernel, feat, tuple(range(per)), k, block),
        args, [VMEM] * len(args), VMEM, shape((quarter, LANES), BF16),
        [], 2 * half_flops, 2 * half_bytes,
    )
    squares, turned = call(
        functools.partial(turn_kernel, feat), a, [VMEM] * feat, [VMEM, VMEM],
        [shape((SUB, LANES), F32), shape((width, tokens), BF16)],
        [], 2 * tokens * width, 4 * half_bytes,
    )
    pre_parts = exchange(vals)

    vals = []
    for n, groups in enumerate(halves):
        first, last = n == 0, n == len(halves) - 1
        args = (*e[n * per_half : (n + 1) * per_half], dec_weight, tgt, *vals, *([squares] if last else []))
        vals = [
            call(
                functools.partial(
                    code_grad_kernel, per_half, groups, k, block, first, last, tokens * width
                ),
                args, [VMEM] * len(args), VMEM, shape((quarter, LANES), BF16 if last else F32),
                [], half_flops, half_bytes,
            )
        ]
    grad_parts = exchange(vals[0])

    def out_scratch(rows, columns, block):
        return [pltpu.VMEM((rows, columns), BF16), pltpu.SemaphoreType.DMA((feat_dev // block,))]

    args = (*e, *pre_parts, *inv, squares)
    dec_grad = call(
        functools.partial(dec_grad_kernel, feat, n_layer, LANES, tokens * width),
        args, [VMEM] * len(args), ANY, shape((1, feat_dev, width), BF16),
        out_scratch(feat_dev, width, LANES), 2 * half_flops, 2 * feat_dev * width,
    )
    args = (*grad_parts, turned, *inv)
    enc_grad = call(
        functools.partial(enc_grad_kernel, n_layer, block, min(512, width)),
        args, [VMEM] * len(args), ANY, shape((1, width, feat_dev), BF16),
        out_scratch(width, feat_dev, block), 2 * half_flops, 2 * feat_dev * width,
    )
    return (dec_grad, enc_grad)


def partner(d, s, count):
    return d ^ s if count & (count - 1) == 0 else (d + s) % count


def steps_of(outer):
    return outer // 2, outer - 1 - outer // 2


def solution(mesh):
    feat, n_layer = mesh.shape["feat"], mesh.shape["layer"]
    inner = 2 if feat % 2 == 0 else 1

    return jax.shard_map(
        functools.partial(on_device_ops, feat // inner, inner, n_layer),
        mesh=mesh,
        in_specs=(
            P("layer", "feat", None),
            P("layer", "feat", None),
            P("layer", None, "feat"),
            P("layer", "feat", None),
            P(),
        ),
        out_specs=(P("layer", "feat", None), P("layer", None, "feat")),
        check_vma=False,
    )
```

```python
import functools

import jax
import jax.numpy as jnp
from jax import lax
from jax.experimental import pallas as pl
from jax.experimental.pallas import tpu as pltpu
from jax.sharding import PartitionSpec as P


LANES = 128
VECTOR_FLOPS = 1024
SUB = 8
F32 = jnp.float32
BF16 = jnp.bfloat16


def lanes_of(x, index):
    numbers = lax.GatherDimensionNumbers(
        offset_dims=(),
        collapsed_slice_dims=(1,),
        start_index_map=(1,),
        operand_batching_dims=(0,),
        start_indices_batching_dims=(0,),
    )
    return lax.gather(
        x, index[..., None], numbers, slice_sizes=(1, 1), mode=lax.GatherScatterMode.PROMISE_IN_BOUNDS
    )


def pack_kernel(starts, chosen, tgt, held):
    k, tokens = chosen.shape
    quarter = tgt.shape[0]
    n_chunks = starts.shape[0] - 1
    rows = tokens // n_chunks
    held[:, :k] = chosen[...].T - starts[0]
    for p in range(n_chunks):
        q, r0 = divmod(p * rows, quarter)
        tgt[r0 : r0 + rows, q * k : (q + 1) * k] = held[pl.ds(pl.multiple_of(starts[1 + p], SUB), rows), :k]


def index_kernel(k, groups, tgt, inv):
    width = inv.shape[1]
    quarter = tgt.shape[0]
    column = lax.broadcasted_iota(jnp.int32, (SUB, width), 1)

    def body(m, _):
        ids = tgt[pl.ds(pl.multiple_of(m * SUB, SUB), SUB), :]
        for n, q in enumerate(groups):
            out = jnp.full((SUB, width), -1, jnp.int32)
            for j in range(k):
                lane = q * k + j
                out = jnp.where(ids[:, lane : lane + 1] == column, lane, out)
            inv[pl.ds(pl.multiple_of(n * quarter + m * SUB, SUB), SUB), :] = out
        return 0

    lax.fori_loop(0, quarter // SUB, body, 0)


def pick(dense, ids, out, groups, first_block, k):
    width = dense.shape[1]
    per = LANES // k
    quarter = ids.shape[0]
    lane_group = lax.broadcasted_iota(jnp.int32, (SUB, LANES), 1) // k
    blocks = width // LANES
    picked = []
    for m in range(quarter // SUB):
        want = ids[m * SUB : (m + 1) * SUB, :]
        low = jnp.bitwise_and(want, LANES - 1)
        key = jnp.right_shift(want, 7) * per + lane_group
        value = out[m]
        for h in range(blocks):
            for q in groups:
                t = (q - groups[0]) * quarter + m * SUB
                got = lanes_of(dense[t : t + SUB, h * LANES : (h + 1) * LANES], low)
                value = jnp.where(key == (first_block + h) * per + q, got, value)
        picked.append(value)
    return picked


def expand(vals, inv, first, size):
    tokens = inv.shape[0]
    quarter = vals[0].shape[0] * len(vals)
    rows_out = []
    for t in range(0, tokens, SUB):
        source = vals[t % quarter // SUB]
        parts = []
        for h in range(size // LANES):
            at = inv[t : t + SUB, first + h * LANES : first + (h + 1) * LANES]
            got = lanes_of(source, jnp.bitwise_and(at, LANES - 1))
            parts.append(jnp.where(at >= 0, got, 0.0))
        rows_out.append(jnp.concatenate(parts, axis=1))
    return jnp.concatenate(rows_out, axis=0)


def row_blocks(ref):
    return [ref[m : m + SUB, :] for m in range(0, ref.shape[0], SUB)]


def stacked(chunks):
    return jnp.concatenate([chunk[0] for chunk in chunks], axis=0)


def pre_kernel(n_chunks, groups, k, block, first, *refs):
    refs = list(refs)
    chunks = [refs.pop(0) for _ in range(n_chunks)]
    weight, ids = refs.pop(0), refs.pop(0)
    before = None if first else refs.pop(0)
    (vals,) = refs
    rows = stacked(chunks)
    acc = [jnp.zeros((SUB, LANES), F32)] * (ids.shape[0] // SUB) if first else row_blocks(before)
    for j in range(0, weight.shape[2], block):
        dense = jnp.dot(rows, weight[0, :, j : j + block], preferred_element_type=F32)
        acc = pick(dense, ids, acc, groups, j // LANES, k)
    vals[...] = jnp.concatenate(acc, axis=0).astype(vals.dtype)


def turn_kernel(n_chunks, *refs):
    chunks = refs[:n_chunks]
    squares, turned = refs[n_chunks:]
    rows = stacked(chunks)
    turned[...] = rows.T
    tokens, width = rows.shape
    values = rows.astype(F32)
    total = jnp.sum((values * values).reshape(tokens // SUB, SUB, width), axis=0)
    part = total[:, :LANES]
    for j in range(LANES, width, LANES):
        part = part + total[:, j : j + LANES]
    squares[...] = part


def scale_of(squares, count):
    return 2.0 / (jnp.sum(squares[...]) / count + 1e-6)


def code_grad_kernel(n_chunks, groups, k, block, first, last, count, *refs):
    refs = list(refs)
    chunks = [refs.pop(0) for _ in range(n_chunks)]
    weight, ids = refs.pop(0), refs.pop(0)
    before = None if first else refs.pop(0)
    squares = refs.pop(0) if last else None
    (vals,) = refs
    rows = stacked(chunks)
    quarter = ids.shape[0]
    acc = [jnp.zeros((SUB, LANES), F32)] * (quarter // SUB) if first else row_blocks(before)
    for j in range(0, weight.shape[1], block):
        dense = lax.dot_general(
            rows, weight[0, j : j + block, :], (((1,), (1,)), ((), ())), preferred_element_type=F32
        )
        acc = pick(dense, ids, acc, groups, j // LANES, k)
    out = jnp.concatenate(acc, axis=0)
    if last:
        out = out * scale_of(squares, count)
    vals[...] = out.astype(vals.dtype)


def total_of(parts):
    total = parts[0][...].astype(F32)
    for part in parts[1:]:
        total = total + part[...].astype(F32)
    return total


def split_rows(value):
    return [value[m : m + SUB] for m in range(0, value.shape[0], SUB)]


def dec_grad_kernel(n_chunks, n_parts, block, count, *refs):
    chunks = refs[:n_chunks]
    parts = refs[n_chunks : n_chunks + n_parts]
    *inv, squares, out, held, sems = refs[n_chunks + n_parts :]
    vals = split_rows(total_of(parts) * scale_of(squares, count))
    rows = stacked(chunks)
    copies = []
    for n, j in enumerate(range(0, inv[0].shape[1], block)):
        codes = jnp.concatenate([expand(vals, half, j, block) for half in inv], axis=0).T.astype(BF16)
        held[j : j + block, :] = jnp.dot(codes, rows, preferred_element_type=F32).astype(BF16)
        copies.append(
            pltpu.make_async_copy(held.at[pl.ds(j, block), :], out.at[0, pl.ds(j, block), :], sems.at[n])
        )
        copies[-1].start()
    for copy in copies:
        copy.wait()


def enc_grad_kernel(n_parts, block, tall, *refs):
    parts = refs[:n_parts]
    turned, *inv, out, held, sems = refs[n_parts:]
    vals = split_rows(total_of(parts))
    copies = []
    for n, j in enumerate(range(0, inv[0].shape[1], block)):
        pre_grad = jnp.concatenate([expand(vals, half, j, block) for half in inv], axis=0).astype(BF16)
        for m in range(0, turned.shape[0], tall):
            held[m : m + tall, j : j + block] = jnp.dot(
                turned[m : m + tall, :], pre_grad, preferred_element_type=F32
            ).astype(BF16)
        copies.append(
            pltpu.make_async_copy(held.at[:, pl.ds(j, block)], out.at[0, :, pl.ds(j, block)], sems.at[n])
        )
        copies[-1].start()
    for copy in copies:
        copy.wait()


VMEM = pl.BlockSpec(memory_space=pltpu.VMEM)
SMEM = pl.BlockSpec(memory_space=pltpu.SMEM)
ANY = pl.BlockSpec(memory_space=pl.ANY)


def call(kernel, args, in_specs, out_specs, out_shape, scratch, flops, nbytes):
    return pl.pallas_call(
        kernel,
        in_specs=in_specs,
        out_specs=out_specs,
        out_shape=out_shape,
        scratch_shapes=scratch,
        compiler_params=pltpu.CompilerParams(vmem_limit_bytes=24 << 20),
        cost_estimate=pl.CostEstimate(
            flops=flops, bytes_accessed=nbytes, transcendentals=0
        ),
    )(*args)


def on_device_ops(outer, inner, n_layer, acts, errors, enc_weight, dec_weight, chosen):
    feat = outer * inner
    rows, width = acts.shape[1], acts.shape[2]
    feat_dev = enc_weight.shape[2]
    tokens, k = chosen.shape
    quarter = tokens // (LANES // k)
    me = lax.axis_index("feat")
    my_outer, my_inner = me // inner, me % inner
    places = [(o, i) for o in range(outer) for i in range(inner)]

    def ring(by):
        return [(o * inner + i, (o + by) % outer * inner + i) for o, i in places]

    def turn(by):
        return [(o * inner + i, o * inner + (i + by) % inner) for o, i in places]

    def send(x, pairs):
        return lax.ppermute(x, "feat", pairs)

    right, left = steps_of(outer)

    def gather(x, last_by_ring):
        fronts, sides = [x], [[send(x, turn(c)) for c in range(1, inner)]]
        for n in range(1, right + 1):
            fronts.append(send(fronts[-1], ring(1)))
            if n == right and last_by_ring:
                sides.append([send(y, ring(1)) for y in sides[-1]])
            else:
                sides.append([send(fronts[-1], turn(c)) for c in range(1, inner)])
        held = x
        for _ in range(1, left + 1):
            held = send(held, ring(-1))
            fronts.append(held)
            sides.append([send(held, turn(c)) for c in range(1, inner)])
        return [y for front, side in zip(fronts, sides) for y in (front, *side)]

    starts = [me * feat_dev]
    for by in [*range(right + 1), *(-n for n in range(1, left + 1))]:
        for c in range(inner):
            o = (my_outer - by + outer) % outer
            i = (my_inner - c + inner) % inner
            starts.append((o * inner + i) * rows)
    starts = jnp.stack(starts).astype(jnp.int32)

    a = gather(acts, False)
    e = gather(errors, True)

    shape = jax.ShapeDtypeStruct
    per = LANES // k
    block = min(256, feat_dev)
    tgt = call(
        pack_kernel, (starts, chosen.T), [SMEM, VMEM], VMEM,
        shape((quarter, LANES), jnp.int32), [pltpu.VMEM((tokens, LANES), jnp.int32)],
        tokens * k, 4 * tokens * LANES,
    )
    halves = [tuple(range(per // 2)), tuple(range(per // 2, per))]
    per_half = feat // 2
    half_tokens = tokens // 2
    half_flops = 2 * half_tokens * width * feat_dev
    half_bytes = 2 * width * half_tokens
    inv = []
    for groups in halves:
        inv.append(
            call(
                functools.partial(index_kernel, k, groups), (tgt,), [VMEM], VMEM,
                shape((half_tokens, feat_dev), jnp.int32), [],
                VECTOR_FLOPS * half_tokens * k * feat_dev, 4 * half_tokens * feat_dev,
            )
        )

    def exchange(value):
        parts = [value]
        for s in range(1, n_layer):
            pairs = [(d, partner(d, s, n_layer)) for d in range(n_layer)]
            parts.append(lax.ppermute(value, "layer", pairs))
        return parts

    vals = []
    for n, groups in enumerate(halves):
        first, last = n == 0, n == len(halves) - 1
        args = (*a[n * per_half : (n + 1) * per_half], enc_weight, tgt, *vals)
        vals = [
            call(
                functools.partial(pre_kernel, per_half, groups, k, block, first),
                args, [VMEM] * len(args), VMEM, shape((quarter, LANES), BF16 if last else F32),
                [], half_flops, half_bytes,
            )
        ]
    squares, turned = call(
        functools.partial(turn_kernel, feat), a, [VMEM] * feat, [VMEM, VMEM],
        [shape((SUB, LANES), F32), shape((width, tokens), BF16)],
        [], 2 * tokens * width, 4 * half_bytes,
    )
    pre_parts = exchange(vals[0])

    vals = []
    for n, groups in enumerate(halves):
        first, last = n == 0, n == len(halves) - 1
        args = (*e[n * per_half : (n + 1) * per_half], dec_weight, tgt, *vals, *([squares] if last else []))
        vals = [
            call(
                functools.partial(
                    code_grad_kernel, per_half, groups, k, block, first, last, tokens * width
                ),
                args, [VMEM] * len(args), VMEM, shape((quarter, LANES), BF16 if last else F32),
                [], half_flops, half_bytes,
            )
        ]
    grad_parts = exchange(vals[0])

    def out_scratch(rows, columns, block):
        return [pltpu.VMEM((rows, columns), BF16), pltpu.SemaphoreType.DMA((feat_dev // block,))]

    args = (*e, *pre_parts, *inv, squares)
    dec_grad = call(
        functools.partial(dec_grad_kernel, feat, n_layer, LANES, tokens * width),
        args, [VMEM] * len(args), ANY, shape((1, feat_dev, width), BF16),
        out_scratch(feat_dev, width, LANES), 2 * half_flops, 2 * feat_dev * width,
    )
    args = (*grad_parts, turned, *inv)
    enc_grad = call(
        functools.partial(enc_grad_kernel, n_layer, block, min(512, width)),
        args, [VMEM] * len(args), ANY, shape((1, width, feat_dev), BF16),
        out_scratch(width, feat_dev, block), 2 * half_flops, 2 * feat_dev * width,
    )
    return (dec_grad, enc_grad)


def partner(d, s, count):
    return d ^ s if count & (count - 1) == 0 else (d + s) % count


def steps_of(outer):
    return outer // 2, outer - 1 - outer // 2


def solution(mesh):
    feat, n_layer = mesh.shape["feat"], mesh.shape["layer"]
    inner = 2 if feat % 2 == 0 else 1

    return jax.shard_map(
        functools.partial(on_device_ops, feat // inner, inner, n_layer),
        mesh=mesh,
        in_specs=(
            P("layer", "feat", None),
            P("layer", "feat", None),
            P("layer", None, "feat"),
            P("layer", "feat", None),
            P(),
        ),
        out_specs=(P("layer", "feat", None), P("layer", None, "feat")),
        check_vma=False,
    )
```

```python
import functools

import jax
import jax.numpy as jnp
from jax import lax
from jax.experimental import pallas as pl
from jax.experimental.pallas import tpu as pltpu
from jax.sharding import PartitionSpec as P


LANES = 128
VECTOR_FLOPS = 1024
SUB = 8
F32 = jnp.float32
BF16 = jnp.bfloat16


def lanes_of(x, index):
    numbers = lax.GatherDimensionNumbers(
        offset_dims=(),
        collapsed_slice_dims=(1,),
        start_index_map=(1,),
        operand_batching_dims=(0,),
        start_indices_batching_dims=(0,),
    )
    return lax.gather(
        x, index[..., None], numbers, slice_sizes=(1, 1), mode=lax.GatherScatterMode.PROMISE_IN_BOUNDS
    )


def pack_kernel(starts, chosen, tgt, held):
    k, tokens = chosen.shape
    quarter = tgt.shape[0]
    n_chunks = starts.shape[0] - 1
    rows = tokens // n_chunks
    held[:, :k] = chosen[...].T - starts[0]
    for p in range(n_chunks):
        q, r0 = divmod(p * rows, quarter)
        tgt[r0 : r0 + rows, q * k : (q + 1) * k] = held[pl.ds(pl.multiple_of(starts[1 + p], SUB), rows), :k]


def index_kernel(k, groups, tgt, inv):
    width = inv.shape[1]
    quarter = tgt.shape[0]
    column = lax.broadcasted_iota(jnp.int32, (SUB, width), 1)

    def body(m, _):
        ids = tgt[pl.ds(pl.multiple_of(m * SUB, SUB), SUB), :]
        for n, q in enumerate(groups):
            out = jnp.full((SUB, width), -1, jnp.int32)
            for j in range(k):
                lane = q * k + j
                out = jnp.where(ids[:, lane : lane + 1] == column, lane, out)
            inv[pl.ds(pl.multiple_of(n * quarter + m * SUB, SUB), SUB), :] = out
        return 0

    lax.fori_loop(0, quarter // SUB, body, 0)


def pick(dense, ids, out, groups, first_block, k):
    width = dense.shape[1]
    per = LANES // k
    quarter = ids.shape[0]
    lane_group = lax.broadcasted_iota(jnp.int32, (SUB, LANES), 1) // k
    blocks = width // LANES
    picked = []
    for m in range(quarter // SUB):
        want = ids[m * SUB : (m + 1) * SUB, :]
        low = jnp.bitwise_and(want, LANES - 1)
        key = jnp.right_shift(want, 7) * per + lane_group
        value = out[m]
        for h in range(blocks):
            for q in groups:
                t = (q - groups[0]) * quarter + m * SUB
                got = lanes_of(dense[t : t + SUB, h * LANES : (h + 1) * LANES], low)
                value = jnp.where(key == (first_block + h) * per + q, got, value)
        picked.append(value)
    return picked


def expand(vals, inv, first, size):
    tokens = inv.shape[0]
    quarter = vals[0].shape[0] * len(vals)
    rows_out = []
    for t in range(0, tokens, SUB):
        source = vals[t % quarter // SUB]
        parts = []
        for h in range(size // LANES):
            at = inv[t : t + SUB, first + h * LANES : first + (h + 1) * LANES]
            got = lanes_of(source, jnp.bitwise_and(at, LANES - 1))
            parts.append(jnp.where(at >= 0, got, 0.0))
        rows_out.append(jnp.concatenate(parts, axis=1))
    return jnp.concatenate(rows_out, axis=0)


def row_blocks(ref):
    return [ref[m : m + SUB, :] for m in range(0, ref.shape[0], SUB)]


def stacked(chunks):
    return jnp.concatenate([chunk[0] for chunk in chunks], axis=0)


def pre_kernel(n_chunks, groups, k, block, first, *refs):
    refs = list(refs)
    chunks = [refs.pop(0) for _ in range(n_chunks)]
    weight, ids = refs.pop(0), refs.pop(0)
    before = None if first else refs.pop(0)
    (vals,) = refs
    rows = stacked(chunks)
    acc = [jnp.zeros((SUB, LANES), F32)] * (ids.shape[0] // SUB) if first else row_blocks(before)
    for j in range(0, weight.shape[2], block):
        dense = jnp.dot(rows, weight[0, :, j : j + block], preferred_element_type=F32)
        acc = pick(dense, ids, acc, groups, j // LANES, k)
    vals[...] = jnp.concatenate(acc, axis=0).astype(vals.dtype)


def turn_kernel(n_chunks, *refs):
    chunks = refs[:n_chunks]
    scale, turned = refs[n_chunks:]
    rows = stacked(chunks)
    turned[...] = rows.T
    tokens, width = rows.shape
    values = rows.astype(F32)
    total = jnp.sum((values * values).reshape(tokens // SUB, SUB, width), axis=0)
    part = total[:, :LANES]
    for j in range(LANES, width, LANES):
        part = part + total[:, j : j + LANES]
    scale[...] = jnp.full(scale.shape, 2.0 / (jnp.sum(part) / (tokens * width) + 1e-6), F32)


def code_grad_kernel(n_chunks, groups, k, block, first, last, *refs):
    refs = list(refs)
    chunks = [refs.pop(0) for _ in range(n_chunks)]
    weight, ids = refs.pop(0), refs.pop(0)
    before = None if first else refs.pop(0)
    scale = refs.pop(0) if last else None
    (vals,) = refs
    rows = stacked(chunks)
    quarter = ids.shape[0]
    acc = [jnp.zeros((SUB, LANES), F32)] * (quarter // SUB) if first else row_blocks(before)
    for j in range(0, weight.shape[1], block):
        dense = lax.dot_general(
            rows, weight[0, j : j + block, :], (((1,), (1,)), ((), ())), preferred_element_type=F32
        )
        acc = pick(dense, ids, acc, groups, j // LANES, k)
    if last:
        acc = [part * scale[...] for part in acc]
    vals[...] = jnp.concatenate(acc, axis=0).astype(vals.dtype)


def total_of(parts):
    total = parts[0][...].astype(F32)
    for part in parts[1:]:
        total = total + part[...].astype(F32)
    return total


def split_rows(value):
    return [value[m : m + SUB] for m in range(0, value.shape[0], SUB)]


def dec_grad_kernel(n_chunks, n_parts, block, *refs):
    chunks = refs[:n_chunks]
    parts = refs[n_chunks : n_chunks + n_parts]
    *inv, scale, out, held, sems = refs[n_chunks + n_parts :]
    vals = [part * scale[...] for part in split_rows(total_of(parts))]
    rows = stacked(chunks)
    copies = []
    for n, j in enumerate(range(0, inv[0].shape[1], block)):
        codes = jnp.concatenate([expand(vals, half, j, block) for half in inv], axis=0).T.astype(BF16)
        held[j : j + block, :] = jnp.dot(codes, rows, preferred_element_type=F32).astype(BF16)
        copies.append(
            pltpu.make_async_copy(held.at[pl.ds(j, block), :], out.at[0, pl.ds(j, block), :], sems.at[n])
        )
        copies[-1].start()
    for copy in copies:
        copy.wait()


def enc_grad_kernel(n_parts, block, tall, *refs):
    parts = refs[:n_parts]
    turned, *inv, out, held, sems = refs[n_parts:]
    vals = split_rows(total_of(parts))
    width, feat_dev = held.shape

    def dense(j):
        return jnp.concatenate([expand(vals, half, j, block) for half in inv], axis=0).astype(BF16)

    copies = []
    pre_grad = dense(0)
    for j in range(0, feat_dev, block):
        last = j + block == feat_dev
        after = None if last else dense(j + block)
        reach = width // 2 if last else width
        for m in range(0, width, tall):
            held[m : m + tall, j : j + block] = jnp.dot(
                turned[m : m + tall, :], pre_grad, preferred_element_type=F32
            ).astype(BF16)
            if (m + tall) % reach == 0:
                part = (pl.ds(m + tall - reach, reach), pl.ds(j, block))
                copies.append(pltpu.make_async_copy(held.at[part], out.at[(0, *part)], sems.at[len(copies)]))
                copies[-1].start()
        pre_grad = after
    for copy in copies:
        copy.wait()


VMEM = pl.BlockSpec(memory_space=pltpu.VMEM)
SMEM = pl.BlockSpec(memory_space=pltpu.SMEM)
ANY = pl.BlockSpec(memory_space=pl.ANY)


def call(kernel, args, in_specs, out_specs, out_shape, scratch, flops, nbytes):
    return pl.pallas_call(
        kernel,
        in_specs=in_specs,
        out_specs=out_specs,
        out_shape=out_shape,
        scratch_shapes=scratch,
        compiler_params=pltpu.CompilerParams(vmem_limit_bytes=24 << 20),
        cost_estimate=pl.CostEstimate(
            flops=flops, bytes_accessed=nbytes, transcendentals=0
        ),
    )(*args)


def on_device_ops(outer, inner, n_layer, acts, errors, enc_weight, dec_weight, chosen):
    feat = outer * inner
    rows, width = acts.shape[1], acts.shape[2]
    feat_dev = enc_weight.shape[2]
    tokens, k = chosen.shape
    quarter = tokens // (LANES // k)
    me = lax.axis_index("feat")
    my_outer, my_inner = me // inner, me % inner
    places = [(o, i) for o in range(outer) for i in range(inner)]

    def ring(by):
        return [(o * inner + i, (o + by) % outer * inner + i) for o, i in places]

    def turn(by):
        return [(o * inner + i, o * inner + (i + by) % inner) for o, i in places]

    def send(x, pairs):
        return lax.ppermute(x, "feat", pairs)

    right, left = steps_of(outer)

    def gather(x, last_by_ring):
        fronts, sides = [x], [[send(x, turn(c)) for c in range(1, inner)]]
        for n in range(1, right + 1):
            fronts.append(send(fronts[-1], ring(1)))
            if n == right and last_by_ring:
                sides.append([send(y, ring(1)) for y in sides[-1]])
            else:
                sides.append([send(fronts[-1], turn(c)) for c in range(1, inner)])
        held = x
        for _ in range(1, left + 1):
            held = send(held, ring(-1))
            fronts.append(held)
            sides.append([send(held, turn(c)) for c in range(1, inner)])
        return [y for front, side in zip(fronts, sides) for y in (front, *side)]

    starts = [me * feat_dev]
    for by in [*range(right + 1), *(-n for n in range(1, left + 1))]:
        for c in range(inner):
            o = (my_outer - by + outer) % outer
            i = (my_inner - c + inner) % inner
            starts.append((o * inner + i) * rows)
    starts = jnp.stack(starts).astype(jnp.int32)

    a = gather(acts, False)
    e = gather(errors, True)

    shape = jax.ShapeDtypeStruct
    per = LANES // k
    block = min(256, feat_dev)
    tgt = call(
        pack_kernel, (starts, chosen.T), [SMEM, VMEM], VMEM,
        shape((quarter, LANES), jnp.int32), [pltpu.VMEM((tokens, LANES), jnp.int32)],
        tokens * k, 4 * tokens * LANES,
    )
    halves = [tuple(range(per // 2)), tuple(range(per // 2, per))]
    per_half = feat // 2
    half_tokens = tokens // 2
    half_flops = 2 * half_tokens * width * feat_dev
    half_bytes = 2 * width * half_tokens
    inv = []
    for groups in halves:
        inv.append(
            call(
                functools.partial(index_kernel, k, groups), (tgt,), [VMEM], VMEM,
                shape((half_tokens, feat_dev), jnp.int32), [],
                VECTOR_FLOPS * half_tokens * k * feat_dev, 4 * half_tokens * feat_dev,
            )
        )

    def exchange(value):
        parts = [value]
        for s in range(1, n_layer):
            pairs = [(d, partner(d, s, n_layer)) for d in range(n_layer)]
            parts.append(lax.ppermute(value, "layer", pairs))
        return parts

    vals = []
    for n, groups in enumerate(halves):
        first, last = n == 0, n == len(halves) - 1
        args = (*a[n * per_half : (n + 1) * per_half], enc_weight, tgt, *vals)
        vals = [
            call(
                functools.partial(pre_kernel, per_half, groups, k, block, first),
                args, [VMEM] * len(args), VMEM, shape((quarter, LANES), BF16 if last else F32),
                [], half_flops, half_bytes,
            )
        ]
    scale, turned = call(
        functools.partial(turn_kernel, feat), a, [VMEM] * feat, [VMEM, VMEM],
        [shape((SUB, LANES), F32), shape((width, tokens), BF16)],
        [], 2 * tokens * width, 4 * half_bytes,
    )
    pre_parts = exchange(vals[0])

    vals = []
    for n, groups in enumerate(halves):
        first, last = n == 0, n == len(halves) - 1
        args = (*e[n * per_half : (n + 1) * per_half], dec_weight, tgt, *vals, *([scale] if last else []))
        vals = [
            call(
                functools.partial(
                    code_grad_kernel, per_half, groups, k, block, first, last
                ),
                args, [VMEM] * len(args), VMEM, shape((quarter, LANES), BF16 if last else F32),
                [], half_flops, half_bytes,
            )
        ]
    grad_parts = exchange(vals[0])

    def out_scratch(rows, columns, block):
        return [pltpu.VMEM((rows, columns), BF16), pltpu.SemaphoreType.DMA((feat_dev // block + 1,))]

    args = (*e, *pre_parts, *inv, scale)
    dec_grad = call(
        functools.partial(dec_grad_kernel, feat, n_layer, LANES),
        args, [VMEM] * len(args), ANY, shape((1, feat_dev, width), BF16),
        out_scratch(feat_dev, width, LANES), 2 * half_flops, 2 * feat_dev * width,
    )
    args = (*grad_parts, turned, *inv)
    enc_grad = call(
        functools.partial(enc_grad_kernel, n_layer, block, min(512, width)),
        args, [VMEM] * len(args), ANY, shape((1, width, feat_dev), BF16),
        out_scratch(width, feat_dev, block), 2 * half_flops, 2 * feat_dev * width,
    )
    return (dec_grad, enc_grad)


def partner(d, s, count):
    return d ^ s if count & (count - 1) == 0 else (d + s) % count


def steps_of(outer):
    return outer // 2, outer - 1 - outer // 2


def solution(mesh):
    feat, n_layer = mesh.shape["feat"], mesh.shape["layer"]
    inner = 2 if feat % 2 == 0 else 1

    return jax.shard_map(
        functools.partial(on_device_ops, feat // inner, inner, n_layer),
        mesh=mesh,
        in_specs=(
            P("layer", "feat", None),
            P("layer", "feat", None),
            P("layer", None, "feat"),
            P("layer", "feat", None),
            P(),
        ),
        out_specs=(P("layer", "feat", None), P("layer", None, "feat")),
        check_vma=False,
    )
```

```python
import functools

import jax
import jax.numpy as jnp
from jax import lax
from jax.experimental import pallas as pl
from jax.experimental.pallas import tpu as pltpu
from jax.sharding import PartitionSpec as P


LANES = 128
VECTOR_FLOPS = 1024
SUB = 8
F32 = jnp.float32
BF16 = jnp.bfloat16


def lanes_of(x, index):
    numbers = lax.GatherDimensionNumbers(
        offset_dims=(),
        collapsed_slice_dims=(1,),
        start_index_map=(1,),
        operand_batching_dims=(0,),
        start_indices_batching_dims=(0,),
    )
    return lax.gather(
        x, index[..., None], numbers, slice_sizes=(1, 1), mode=lax.GatherScatterMode.PROMISE_IN_BOUNDS
    )


def pack_kernel(starts, chosen, tgt, held):
    k, tokens = chosen.shape
    quarter = tgt.shape[0]
    n_chunks = starts.shape[0] - 1
    rows = tokens // n_chunks
    held[:, :k] = chosen[...].T - starts[0]
    for p in range(n_chunks):
        q, r0 = divmod(p * rows, quarter)
        tgt[r0 : r0 + rows, q * k : (q + 1) * k] = held[pl.ds(pl.multiple_of(starts[1 + p], SUB), rows), :k]


def index_kernel(k, groups, tgt, inv):
    width = inv.shape[1]
    quarter = tgt.shape[0]
    column = lax.broadcasted_iota(jnp.int32, (SUB, width), 1)

    def body(m, _):
        ids = tgt[pl.ds(pl.multiple_of(m * SUB, SUB), SUB), :]
        for n, q in enumerate(groups):
            out = jnp.full((SUB, width), -1, jnp.int32)
            for j in range(k):
                lane = q * k + j
                out = jnp.where(ids[:, lane : lane + 1] == column, lane, out)
            inv[pl.ds(pl.multiple_of(n * quarter + m * SUB, SUB), SUB), :] = out
        return 0

    lax.fori_loop(0, quarter // SUB, body, 0)


def pick(dense, ids, out, groups, first_block, k):
    width = dense.shape[1]
    per = LANES // k
    quarter = ids.shape[0]
    lane_group = lax.broadcasted_iota(jnp.int32, (SUB, LANES), 1) // k
    blocks = width // LANES
    picked = []
    for m in range(quarter // SUB):
        want = ids[m * SUB : (m + 1) * SUB, :]
        low = jnp.bitwise_and(want, LANES - 1)
        key = jnp.right_shift(want, 7) * per + lane_group
        value = out[m]
        for h in range(blocks):
            for q in groups:
                t = (q - groups[0]) * quarter + m * SUB
                got = lanes_of(dense[t : t + SUB, h * LANES : (h + 1) * LANES], low)
                value = jnp.where(key == (first_block + h) * per + q, got, value)
        picked.append(value)
    return picked


def expand(vals, inv, first, size):
    tokens = inv.shape[0]
    quarter = vals[0].shape[0] * len(vals)
    rows_out = []
    for t in range(0, tokens, SUB):
        source = vals[t % quarter // SUB]
        parts = []
        for h in range(size // LANES):
            at = inv[t : t + SUB, first + h * LANES : first + (h + 1) * LANES]
            got = lanes_of(source, jnp.bitwise_and(at, LANES - 1))
            parts.append(jnp.where(at >= 0, got, 0.0))
        rows_out.append(jnp.concatenate(parts, axis=1))
    return jnp.concatenate(rows_out, axis=0)


def row_blocks(ref):
    return [ref[m : m + SUB, :] for m in range(0, ref.shape[0], SUB)]


def stacked(chunks):
    return jnp.concatenate([chunk[0] for chunk in chunks], axis=0)


def pre_kernel(n_chunks, groups, k, block, first, *refs):
    refs = list(refs)
    chunks = [refs.pop(0) for _ in range(n_chunks)]
    weight, ids = refs.pop(0), refs.pop(0)
    before = None if first else refs.pop(0)
    (vals,) = refs
    rows = stacked(chunks)
    acc = [jnp.zeros((SUB, LANES), F32)] * (ids.shape[0] // SUB) if first else row_blocks(before)
    for j in range(0, weight.shape[2], block):
        dense = jnp.dot(rows, weight[0, :, j : j + block], preferred_element_type=F32)
        acc = pick(dense, ids, acc, groups, j // LANES, k)
    vals[...] = jnp.concatenate(acc, axis=0).astype(vals.dtype)


def turn_kernel(n_chunks, *refs):
    chunks = refs[:n_chunks]
    squares, turned = refs[n_chunks:]
    rows = stacked(chunks)
    turned[...] = rows.T
    tokens, width = rows.shape
    values = rows.astype(F32)
    total = jnp.sum((values * values).reshape(tokens // SUB, SUB, width), axis=0)
    part = total[:, :LANES]
    for j in range(LANES, width, LANES):
        part = part + total[:, j : j + LANES]
    squares[...] = part


def scale_of(squares, count):
    return 2.0 / (jnp.sum(squares[...]) / count + 1e-6)


def code_grad_kernel(n_chunks, groups, k, block, first, last, count, *refs):
    refs = list(refs)
    chunks = [refs.pop(0) for _ in range(n_chunks)]
    weight, ids = refs.pop(0), refs.pop(0)
    before = None if first else refs.pop(0)
    squares = refs.pop(0) if last else None
    (vals,) = refs
    rows = stacked(chunks)
    quarter = ids.shape[0]
    acc = [jnp.zeros((SUB, LANES), F32)] * (quarter // SUB) if first else row_blocks(before)
    for j in range(0, weight.shape[1], block):
        dense = lax.dot_general(
            rows, weight[0, j : j + block, :], (((1,), (1,)), ((), ())), preferred_element_type=F32
        )
        acc = pick(dense, ids, acc, groups, j // LANES, k)
    out = jnp.concatenate(acc, axis=0)
    if last:
        out = out * scale_of(squares, count)
    vals[...] = out.astype(vals.dtype)


def total_of(parts):
    total = parts[0][...].astype(F32)
    for part in parts[1:]:
        total = total + part[...].astype(F32)
    return total


def split_rows(value):
    return [value[m : m + SUB] for m in range(0, value.shape[0], SUB)]


def dec_grad_kernel(n_chunks, n_parts, block, count, *refs):
    chunks = refs[:n_chunks]
    parts = refs[n_chunks : n_chunks + n_parts]
    *inv, squares, out, held, sems = refs[n_chunks + n_parts :]
    vals = split_rows(total_of(parts) * scale_of(squares, count))
    rows = stacked(chunks)
    copies = []
    for n, j in enumerate(range(0, inv[0].shape[1], block)):
        codes = jnp.concatenate([expand(vals, half, j, block) for half in inv], axis=0).T.astype(BF16)
        held[j : j + block, :] = jnp.dot(codes, rows, preferred_element_type=F32).astype(BF16)
        copies.append(
            pltpu.make_async_copy(held.at[pl.ds(j, block), :], out.at[0, pl.ds(j, block), :], sems.at[n])
        )
        copies[-1].start()
    for copy in copies:
        copy.wait()


def enc_grad_kernel(n_parts, block, tall, *refs):
    parts = refs[:n_parts]
    turned, *inv, out, held, sems = refs[n_parts:]
    vals = split_rows(total_of(parts))
    width, feat_dev = held.shape

    def dense(j):
        return jnp.concatenate([expand(vals, half, j, block) for half in inv], axis=0).astype(BF16)

    copies = []
    pre_grad = dense(0)
    for j in range(0, feat_dev, block):
        last = j + block == feat_dev
        after = None if last else dense(j + block)
        reach = width // 2 if last else width
        for m in range(0, width, tall):
            held[m : m + tall, j : j + block] = jnp.dot(
                turned[m : m + tall, :], pre_grad, preferred_element_type=F32
            ).astype(BF16)
            if (m + tall) % reach == 0:
                part = (pl.ds(m + tall - reach, reach), pl.ds(j, block))
                copies.append(pltpu.make_async_copy(held.at[part], out.at[(0, *part)], sems.at[len(copies)]))
                copies[-1].start()
        pre_grad = after
    for copy in copies:
        copy.wait()


VMEM = pl.BlockSpec(memory_space=pltpu.VMEM)
SMEM = pl.BlockSpec(memory_space=pltpu.SMEM)
ANY = pl.BlockSpec(memory_space=pl.ANY)


def call(kernel, args, in_specs, out_specs, out_shape, scratch, flops, nbytes):
    return pl.pallas_call(
        kernel,
        in_specs=in_specs,
        out_specs=out_specs,
        out_shape=out_shape,
        scratch_shapes=scratch,
        compiler_params=pltpu.CompilerParams(vmem_limit_bytes=24 << 20),
        cost_estimate=pl.CostEstimate(
            flops=flops, bytes_accessed=nbytes, transcendentals=0
        ),
    )(*args)


def on_device_ops(outer, inner, n_layer, acts, errors, enc_weight, dec_weight, chosen):
    feat = outer * inner
    rows, width = acts.shape[1], acts.shape[2]
    feat_dev = enc_weight.shape[2]
    tokens, k = chosen.shape
    quarter = tokens // (LANES // k)
    me = lax.axis_index("feat")
    my_outer, my_inner = me // inner, me % inner
    places = [(o, i) for o in range(outer) for i in range(inner)]

    def ring(by):
        return [(o * inner + i, (o + by) % outer * inner + i) for o, i in places]

    def turn(by):
        return [(o * inner + i, o * inner + (i + by) % inner) for o, i in places]

    def send(x, pairs):
        return lax.ppermute(x, "feat", pairs)

    right, left = steps_of(outer)

    def gather(x, last_by_ring):
        fronts, sides = [x], [[send(x, turn(c)) for c in range(1, inner)]]
        for n in range(1, right + 1):
            fronts.append(send(fronts[-1], ring(1)))
            if n == right and last_by_ring:
                sides.append([send(y, ring(1)) for y in sides[-1]])
            else:
                sides.append([send(fronts[-1], turn(c)) for c in range(1, inner)])
        held = x
        for _ in range(1, left + 1):
            held = send(held, ring(-1))
            fronts.append(held)
            sides.append([send(held, turn(c)) for c in range(1, inner)])
        return [y for front, side in zip(fronts, sides) for y in (front, *side)]

    starts = [me * feat_dev]
    for by in [*range(right + 1), *(-n for n in range(1, left + 1))]:
        for c in range(inner):
            o = (my_outer - by + outer) % outer
            i = (my_inner - c + inner) % inner
            starts.append((o * inner + i) * rows)
    starts = jnp.stack(starts).astype(jnp.int32)

    a = gather(acts, False)
    e = gather(errors, True)

    shape = jax.ShapeDtypeStruct
    per = LANES // k
    block = min(256, feat_dev)
    tgt = call(
        pack_kernel, (starts, chosen.T), [SMEM, VMEM], VMEM,
        shape((quarter, LANES), jnp.int32), [pltpu.VMEM((tokens, LANES), jnp.int32)],
        tokens * k, 4 * tokens * LANES,
    )
    halves = [tuple(range(per // 2)), tuple(range(per // 2, per))]
    per_half = feat // 2
    half_tokens = tokens // 2
    half_flops = 2 * half_tokens * width * feat_dev
    half_bytes = 2 * width * half_tokens
    inv = []
    for groups in halves:
        inv.append(
            call(
                functools.partial(index_kernel, k, groups), (tgt,), [VMEM], VMEM,
                shape((half_tokens, feat_dev), jnp.int32), [],
                VECTOR_FLOPS * half_tokens * k * feat_dev, 4 * half_tokens * feat_dev,
            )
        )

    def exchange(value):
        parts = [value]
        for s in range(1, n_layer):
            pairs = [(d, partner(d, s, n_layer)) for d in range(n_layer)]
            parts.append(lax.ppermute(value, "layer", pairs))
        return parts

    vals = []
    for n, groups in enumerate(halves):
        first, last = n == 0, n == len(halves) - 1
        args = (*a[n * per_half : (n + 1) * per_half], enc_weight, tgt, *vals)
        vals = [
            call(
                functools.partial(pre_kernel, per_half, groups, k, block, first),
                args, [VMEM] * len(args), VMEM, shape((quarter, LANES), BF16 if last else F32),
                [], half_flops, half_bytes,
            )
        ]
    squares, turned = call(
        functools.partial(turn_kernel, feat), a, [VMEM] * feat, [VMEM, VMEM],
        [shape((SUB, LANES), F32), shape((width, tokens), BF16)],
        [], 2 * tokens * width, 4 * half_bytes,
    )
    pre_parts = exchange(vals[0])

    vals = []
    for n, groups in enumerate(halves):
        first, last = n == 0, n == len(halves) - 1
        args = (*e[n * per_half : (n + 1) * per_half], dec_weight, tgt, *vals, *([squares] if last else []))
        vals = [
            call(
                functools.partial(
                    code_grad_kernel, per_half, groups, k, block, first, last, tokens * width
                ),
                args, [VMEM] * len(args), VMEM, shape((quarter, LANES), BF16 if last else F32),
                [], half_flops, half_bytes,
            )
        ]
    grad_parts = exchange(vals[0])

    def out_scratch(rows, columns, block):
        return [pltpu.VMEM((rows, columns), BF16), pltpu.SemaphoreType.DMA((feat_dev // block + 1,))]

    args = (*e, *pre_parts, *inv, squares)
    dec_grad = call(
        functools.partial(dec_grad_kernel, feat, n_layer, LANES, tokens * width),
        args, [VMEM] * len(args), ANY, shape((1, feat_dev, width), BF16),
        out_scratch(feat_dev, width, LANES), 2 * half_flops, 2 * feat_dev * width,
    )
    args = (*grad_parts, turned, *inv)
    enc_grad = call(
        functools.partial(enc_grad_kernel, n_layer, block, min(512, width)),
        args, [VMEM] * len(args), ANY, shape((1, width, feat_dev), BF16),
        out_scratch(width, feat_dev, block), 2 * half_flops, 2 * feat_dev * width,
    )
    return (dec_grad, enc_grad)


def partner(d, s, count):
    return d ^ s if count & (count - 1) == 0 else (d + s) % count


def steps_of(outer):
    return outer // 2, outer - 1 - outer // 2


def solution(mesh):
    feat, n_layer = mesh.shape["feat"], mesh.shape["layer"]
    inner = 2 if feat % 2 == 0 else 1

    return jax.shard_map(
        functools.partial(on_device_ops, feat // inner, inner, n_layer),
        mesh=mesh,
        in_specs=(
            P("layer", "feat", None),
            P("layer", "feat", None),
            P("layer", None, "feat"),
            P("layer", "feat", None),
            P(),
        ),
        out_specs=(P("layer", "feat", None), P("layer", None, "feat")),
        check_vma=False,
    )
```
